128 devices in a mesh: ctx: 16 (over z_hi, x, core), head: 8 (over z_lo, y).
Axes of the slice: x: 4, y: 4, z: 4 (z_hi: 2, z_lo: 2; z = z_hi * 2 + z_lo), core: 2. Of those that a mesh axis runs over, the one named last changes fastest.
Arguments:
- tokens: bfloat16 [16384, 4096], P('ctx', 'head'), may hold values from -23 to 23
- proj_weight: bfloat16 [4096, 32, 384], P(None, 'head'), may hold values from -1 to 1
- partner_shard: int32 [32, 256, 3], P('head'), may hold values from 0 to 15, all different within a row; in each aligned block of 16 rows (0 to 15, 16 to 31, ..., all dimensions but the last counted through in order) at most 6 rows name the same one
- partner_block: int32 [32, 256, 3], P('head'), may hold values from 0 to 15
Outputs:
- attended: bfloat16 [16384, 32, 128], P('ctx', 'head')
The draws below stay inside these ranges and needn't reach their ends.
Inputs may be any that keep to these rules, and one draw needn't show every extreme that they name: `partner_shard`: the 3 entries of one row differ. For each head, within each aligned run of 16 block rows, no value is named more than 6 times, and some runs name one value exactly 6 times.
All inputs are finite; a program needn't handle non-finite values.
Results may differ from the reference program's by a relative error of at most 0.008.
Values may be sent and summed in bfloat16 or wider, within the bound.
A program may use at most 192 MiB of HBM per device.

```python
import math
import jax
import jax.numpy as jnp
import numpy as np
from jax import lax

D = 4096
NH = 32
HEAD_DIMENSION = 128
BLK = 64
GLOB = 2
RAND = 3
BPD = 16
SEQUENCE_TOKENS = 16384
NB = 256
MOST = 6
N_CTX = 16


def draw_tokens(key, part):
    key_base = jax.random.fold_in(jax.random.fold_in(key, 11), 0)
    values = jax.random.truncated_normal(key_base, -4.0, 4.0, (SEQUENCE_TOKENS, D), jnp.float32)
    return values.astype(jnp.bfloat16)


def draw_proj_weight(key, part):
    values = jax.random.truncated_normal(jax.random.fold_in(key, 23), -4.0, 4.0, (D, NH, 3 * HEAD_DIMENSION), jnp.float32) * D ** (-0.5)
    return values.astype(jnp.bfloat16)


def plant(drawn, stream_key, least, high):
    place = [jax.random.randint(jax.random.fold_in(stream_key, axis), (), 0, length) for axis, length in enumerate(drawn.shape)]
    main_axis = drawn.shape.index(max(drawn.shape))
    beside = place[:main_axis] + [(place[main_axis] + 1) % drawn.shape[main_axis]] + place[main_axis + 1:]
    return drawn.at[tuple(place)].set(least).at[tuple(beside)].set(high)


def routed_block(rng, own, number, rows, number_of, top, most, lean):
    order = jax.random.permutation(rng, number_of)
    heavy_load, usual = portions_of(number_of, rows * top, most, lean, True), portions_of(number_of, rows * top, most, lean, False)
    places = jnp.arange(number_of)

    def named(tallies, rotation):
        used = int((tallies > 0).sum())
        fixed = max(1, used // 4)
        shifted = fixed + (places - fixed + rotation * (used - fixed)) % max(1, number_of - fixed)
        return jnp.zeros((number_of,), jnp.int32).at[order[jnp.where(places < fixed, places, shifted)]].set(jnp.asarray(tallies, jnp.int32))

    tallies = jnp.where(number % 4 == 0, named(heavy_load, number // 4), named(usual, number - number // 4 - 1))
    mixed = jax.random.permutation(jax.random.fold_in(own, 3), number_of)
    giver, taker = mixed[0:number_of // 2 * 2:2], mixed[1:number_of // 2 * 2:2]
    slack = jnp.minimum(tallies[giver] - 1, most - tallies[taker]) // 2
    slack = jnp.where((giver == order[0]) | (taker == order[0]) | (tallies[taker] == 0), 0, jnp.maximum(slack, 0))
    shifted = jax.random.randint(jax.random.fold_in(own, 4), (number_of // 2,), 0, 1 << 20) % (slack + 1)
    tallies = tallies.at[giver].add(-shifted).at[taker].add(shifted)
    items = jnp.searchsorted(jnp.cumsum(tallies), jnp.arange(rows * top), side="right").astype(jnp.int32)
    table = items.reshape(top, rows).T
    table = table[jax.random.permutation(jax.random.fold_in(own, 1), rows)]
    rotation = jax.random.randint(jax.random.fold_in(own, 2), (rows, 1), 0, top)
    return jnp.take_along_axis(table, (jnp.arange(top)[None, :] + rotation) % top, axis=1)


def portions_of(number_of, total, most, slope, full):
    portions = [(1 << 20) // math.isqrt(standing ** slope) + 1 for standing in range(1, number_of + 1)]
    largest = most if full else min(most, max(-(-total // number_of), total * portions[0] // sum(portions)))
    least = 1 if total - largest >= number_of - 1 else 0
    holding, rest = [largest] + [least] * (number_of - 1), total - largest - least * (number_of - 1)
    while rest > 0:
        candidates = [i for i in range(1, number_of) if holding[i] < largest] or [i for i in range(1, number_of) if holding[i] < most]
        mass, budget = sum([portions[i] for i in candidates]), rest
        for i in candidates:
            extra = min(most - holding[i], max(1, budget * portions[i] // mass), rest)
            holding[i] = holding[i] + extra
            rest = rest - extra
    return np.array(holding)


def setup_inputs(seed: int = 0) -> dict:
    arg_keys = jax.random.split(jax.random.key(seed), 5)
    tokens = draw_tokens(jax.random.fold_in(arg_keys[4], 71), 0)
    proj_weight = draw_proj_weight(jax.random.fold_in(arg_keys[4], 71), 0)
    partner_shard_keys = jax.random.split(jax.random.fold_in(arg_keys[2], 1), NH * NB // BPD)
    partner_shard_turns = jax.random.permutation(jax.random.fold_in(arg_keys[2], 3), NH * NB // BPD)
    partner_shard = jax.vmap(lambda own, number: routed_block(jax.random.fold_in(arg_keys[2], 2), own, number, BPD, N_CTX, RAND, MOST, 2))(partner_shard_keys, partner_shard_turns).reshape((NH, NB, RAND))
    partner_block = plant(jax.random.randint(arg_keys[3], (NH, NB, RAND), 0, BPD), jax.random.fold_in(arg_keys[3], 1), 0, BPD - 1).astype(jnp.int32)
    return {"tokens": tokens, "proj_weight": proj_weight, "partner_shard": partner_shard, "partner_block": partner_block}


def reference(tokens, proj_weight, partner_shard, partner_block):
    flat_weight = proj_weight.reshape(D, NH * 3 * HEAD_DIMENSION)
    packed = jnp.dot(tokens, flat_weight, preferred_element_type=jnp.float32).astype(jnp.bfloat16)
    packed = jnp.transpose(packed.reshape(SEQUENCE_TOKENS, NH, 3 * HEAD_DIMENSION), (1, 0, 2))
    partner = (partner_shard * BPD + partner_block).astype(jnp.int32)
    inverse_root_scale = HEAD_DIMENSION ** -0.5

    def one_head(inputs):
        head_pack, indices = inputs
        head_pack = head_pack.astype(jnp.float32)
        queries = head_pack[:, :HEAD_DIMENSION]
        keys = head_pack[:, HEAD_DIMENSION:2 * HEAD_DIMENSION]
        values = head_pack[:, 2 * HEAD_DIMENSION:]
        blocked_query_rows = queries.reshape(NB, BLK, HEAD_DIMENSION)

        def gather_set(field):
            field_blocks = field.reshape(NB, BLK, HEAD_DIMENSION)
            leading = jnp.broadcast_to(field_blocks[:GLOB].reshape(1, GLOB * BLK, HEAD_DIMENSION), (NB, GLOB * BLK, HEAD_DIMENSION))
            partners = field_blocks[indices].reshape(NB, RAND * BLK, HEAD_DIMENSION)
            return jnp.concatenate([jnp.roll(field_blocks, 1, 0), field_blocks, jnp.roll(field_blocks, -1, 0), leading, partners], axis=1)

        partner_key_rows = gather_set(keys)
        partner_value_rows = gather_set(values)
        logit_scores = jnp.einsum("msx,mix->msi", blocked_query_rows, partner_key_rows, precision=lax.Precision.HIGHEST) * inverse_root_scale
        softmax_weight_matrix = jax.nn.softmax(logit_scores, axis=-1).astype(jnp.bfloat16)
        softmax_weight_matrix = lax.optimization_barrier(softmax_weight_matrix).astype(jnp.float32)
        sparse_attention_output = jnp.einsum("thw,twp->thp", softmax_weight_matrix, partner_value_rows, precision=lax.Precision.HIGHEST).reshape(SEQUENCE_TOKENS, HEAD_DIMENSION)
        global_scores = jnp.dot(queries[:GLOB * BLK], keys.T, precision=lax.Precision.HIGHEST) * inverse_root_scale
        global_weights = jax.nn.softmax(global_scores, axis=-1)
        global_out = jnp.dot(global_weights, values, precision=lax.Precision.HIGHEST)
        context = jnp.concatenate([global_out, sparse_attention_output[GLOB * BLK:]], axis=0)
        return context.astype(jnp.bfloat16)

    result = lax.map(one_head, (packed, partner))
    return jnp.transpose(result, (1, 0, 2))
```

```python
import functools

import jax
import jax.numpy as jnp
from jax import lax
from jax.experimental import pallas as pl
from jax.experimental.pallas import tpu as pltpu
from jax.sharding import PartitionSpec as P

MESH = pl.DeviceIdType.MESH
HD = 128
BLK = 64
NB = 256
RUN = 1024
TB = 128
T = RUN // TB
LEAD = 5
GROUP = 256
GROUPS = RUN // GROUP
SCALE2 = HD**-0.5 * 1.4426950408889634


def kernel(
    x_ref, w_ref, ps_ref, pb_ref, o_ref,
    xg, wst, wv, qst, kvst, qmy, kv, gq, gm, gl, gacc, gout, grecv, ost,
    x_sem, w_sem, ag_s, ag_r, q_s, q_r, kva_s, kva_r, kvz_s, kvb_r, kvc_s, kvc_r,
    gq_s, gq_r, go_s, go_r, o_s, o_r,
):
    ctx, head = lax.axis_index("ctx"), lax.axis_index("head")
    zh, x, core = ctx // 8, (ctx // 2) % 4, ctx % 2
    zl, y = head // 4, head % 4

    def dev(zh=zh, x=x, core=core, zl=zl, y=y):
        return (zh * 8 + x * 2 + core, zl * 4 + y)

    def run_of(zh, x, core):
        return zh * 8 + x * 2 + core

    up, down = (y + 1) % 4, (y + 3) % 4
    dev_up, dev_down = dev(y=up), dev(y=down)
    dev_zl, dev_zh, dev_core = dev(zl=1 - zl), dev(zh=1 - zh), dev(core=1 - core)

    def remote(src, dst, send, recv, device):
        return pltpu.make_async_remote_copy(
            src_ref=src, dst_ref=dst, send_sem=send, recv_sem=recv,
            device_id=device, device_id_type=MESH,
        )

    own_copy = pltpu.make_async_copy(x_ref, xg.at[head], x_sem.at[0])
    own_copy.start()

    def w_copy(piece, slot):
        return pltpu.make_async_copy(
            w_ref.at[pl.ds(piece * 512, 512)], wst.at[slot], w_sem.at[slot]
        )

    w_copy(0, 0).start()
    w_copy(1, 1).start()

    barrier = pltpu.get_barrier_semaphore()
    for device in (dev_up, dev_down, dev_zl):
        pl.semaphore_signal(barrier, inc=1, device_id=device, device_id_type=MESH)
    for step in range(1, 16):
        pl.semaphore_signal(
            barrier, inc=1, device_id=((ctx + step) % 16, head), device_id_type=MESH
        )
    pl.semaphore_wait(barrier, 18)
    own_copy.wait()

    def xs_at(slot, t):
        return xg.at[slot, pl.ds(pl.multiple_of(t * TB, TB), TB)]

    def ag(kind, slot, t, device):
        return remote(xs_at(slot, t), xs_at(slot, t), ag_s.at[kind, t], ag_r.at[slot, t], device)

    other = (1 - zl) * 4

    def fwd(t):
        forward = t % 2 == 0
        own_slot = zl * 4 + jnp.where(forward, down, up)
        own_dev = jnp.where(forward, up, down)
        far_slot = other + jnp.where(forward, up, down)
        far_dev = jnp.where(forward, down, up)
        return (
            ag(5, own_slot, t, dev(y=own_dev)),
            ag(6, far_slot, t, dev(y=far_dev)),
        )

    def step1(t):
        ag(0, head, t, dev_zl).start()
        ag(1, head, t, dev_up).start()
        ag(2, head, t, dev_down).start()

    def step2(t):
        ag(0, other + y, t, dev_zl).wait_recv()
        ag(3, other + y, t, dev_up).start()
        ag(4, other + y, t, dev_down).start()

    def step3(t):
        for base in (zl * 4, other):
            for side in (up, down):
                ag(1, base + side, t, dev_up).wait_recv()
        a, b = fwd(t)
        a.start()
        b.start()

    def project(t):
        for base in (zl * 4, other):
            ag(5, base + (y + 2) % 4, t, dev_up).wait_recv()
        rows = pl.ds(pl.multiple_of(t * TB, TB), TB)
        blocks = pl.ds(t * (TB // BLK), TB // BLK)
        for n in range(6):
            acc = jnp.dot(
                xg[0, rows], wv[0:512, n * 256 : (n + 1) * 256],
                preferred_element_type=jnp.float32,
            )
            for g in range(1, 8):
                acc = acc + jnp.dot(
                    xg[g, rows], wv[g * 512 : (g + 1) * 512, n * 256 : (n + 1) * 256],
                    preferred_element_type=jnp.float32,
                )
            acc = acc.astype(jnp.bfloat16)
            if n < 2:
                qst[2 * n, rows] = acc[:, :HD]
                qst[2 * n + 1, rows] = acc[:, HD:]
            else:
                kvst[n - 2, blocks] = acc.reshape(TB // BLK, BLK, 2 * HD)

    def kv_at(zs, xs, cs, t):
        start = run_of(zs, xs, cs) * (RUN // BLK) + t * (TB // BLK)
        return kv.at[pl.ds(start, TB // BLK)]

    def q_send(j, t):
        h = (x + j) % 4
        rows = pl.ds(pl.multiple_of(t * TB, TB), TB)
        if j == 0:
            return pltpu.make_async_copy(qst.at[h, rows], qmy.at[x, rows], q_r.at[x, t])
        return remote(qst.at[h, rows], qmy.at[x, rows], q_s.at[j, t], q_r.at[x, t], dev(x=h))

    def kv_send(j, t):
        h = (x + j) % 4
        rows = pl.ds(t * (TB // BLK), TB // BLK)
        dst = kv_at(zh, x, core, t)
        if j == 0:
            return pltpu.make_async_copy(kvst.at[h, rows], dst, kva_r.at[x, t])
        return remote(kvst.at[h, rows], dst, kva_s.at[j, t], kva_r.at[x, t], dev(x=h))

    def gq_copy(target):
        h = (target // 2) % 4
        part = (target // 8) * 2 + target % 2
        src = qst.at[h, pl.ds(pl.multiple_of(part * 32, 32), 32)]
        if target == 0:
            return pltpu.make_async_copy(src, gq, gq_r.at[0])
        return remote(src, gq, gq_s.at[target], gq_r.at[0], (jnp.int32(target), head))

    def send1(t):
        for j in (2, 1, 3, 0):
            kv_send(j, t).start()
        for j in (2, 1, 3, 0):
            q_send(j, t).start()

        @pl.when((t == 0) & (ctx == 0))
        def _():
            for target in range(16):
                gq_copy(target).start()

    def z_fwd(xs, t):
        return remote(
            kv_at(zh, xs, core, t), kv_at(zh, xs, core, t),
            kvz_s.at[xs, t], kvb_r.at[xs, t], dev_zh,
        )

    def c_fwd(zs, z_slot, xs, t):
        return remote(
            kv_at(zs, xs, core, t), kv_at(zs, xs, core, t),
            kvc_s.at[z_slot * 4 + xs, t], kvc_r.at[z_slot * 4 + xs, t], dev_core,
        )

    def send2(t):
        for j in (0, 1, 3, 2):
            xs = (x + j) % 4
            rows = pl.ds(0, TB // BLK)
            pltpu.make_async_copy(kvst.at[0, rows], kv_at(zh, xs, core, t), kva_r.at[xs, t]).wait()
            z_fwd(xs, t).start()
            c_fwd(zh, 0, xs, t).start()

    def send3(t):
        for j in (0, 1, 3, 2):
            xs = (x + j) % 4
            remote(
                kv_at(zh, xs, core, t), kv_at(1 - zh, xs, core, t),
                kvz_s.at[xs, t], kvb_r.at[xs, t], dev_zh,
            ).wait_recv()
            c_fwd(1 - zh, 1, xs, t).start()

    def global_part(t):
        @pl.when(t == 0)
        def _():
            pltpu.make_async_copy(qst.at[0, pl.ds(0, 32)], gq, gq_r.at[0]).wait()
            gm[...] = jnp.full_like(gm, -1e30)
            gl[...] = jnp.zeros_like(gl)
            gacc[...] = jnp.zeros_like(gacc)

        for zslot in range(2):
            for xs in range(4):
                zs = zh if zslot == 0 else 1 - zh
                remote(
                    kv_at(zs, xs, core, t), kv_at(zs, xs, 1 - core, t),
                    kvc_s.at[zslot * 4 + xs, t], kvc_r.at[zslot * 4 + xs, t], dev_core,
                ).wait_recv()
        query = gq[...]
        for quarter in range(4):
            block = jnp.concatenate(
                [
                    kv[pl.ds((quarter * 4 + c) * (RUN // BLK) + t * (TB // BLK), TB // BLK)]
                    for c in range(4)
                ],
                axis=0,
            ).reshape(4 * TB, 2 * HD)
            s = lax.dot_general(
                query, block[:, :HD], (((1,), (1,)), ((), ())),
                preferred_element_type=jnp.float32,
            )
            old = gm[...]
            new = jnp.maximum(old, jnp.max(s, axis=1, keepdims=True))
            factor = jnp.exp2((old - new) * SCALE2)
            e = jnp.exp2((s - new[:, :1]) * SCALE2)
            gm[...] = new
            gl[...] = gl[...] * factor + jnp.sum(e, axis=1, keepdims=True)
            gacc[...] = gacc[...] * factor + jnp.dot(
                e.astype(jnp.bfloat16), block[:, HD:], preferred_element_type=jnp.float32
            )

    for t in range(LEAD):
        step1(t)

    @pl.loop(0, 4)
    def _(pair):
        for slot in range(2):
            piece = pair * 2 + slot
            w_copy(piece, slot).wait()
            for sub in range(4):
                v = jnp.swapaxes(wst[slot, sub * 128 : (sub + 1) * 128], 0, 1)
                rows = pl.ds(pl.multiple_of(piece * 512 + sub * 128, 128), 128)
                for h in range(4):
                    wv[rows, h * HD : (h + 1) * HD] = v[h][:, :HD]
                    wv[rows, 512 + h * 256 : 512 + (h + 1) * 256] = v[h][:, HD:]

            @pl.when(piece + 2 < 8)
            def _():
                w_copy(piece + 2, slot).start()

    step2(0)
    step2(1)
    step3(0)

    @pl.loop(0, T + 3)
    def _(i):
        @pl.when(i + LEAD < T)
        def _():
            step1(i + LEAD)

        @pl.when(i + 2 < T)
        def _():
            step2(i + 2)

        @pl.when(i + 1 < T)
        def _():
            step3(i + 1)

        @pl.when(i < T)
        def _():
            project(i)

        @pl.when((i >= 1) & (i - 1 < T))
        def _():
            send2(i - 1)

        @pl.when((i >= 2) & (i - 2 < T))
        def _():
            send3(i - 2)

        @pl.when(i < T)
        def _():
            send1(i)

        @pl.when(i >= 3)
        def _():
            global_part(i - 3)

    gout[...] = (gacc[...] / gl[...]).astype(jnp.bfloat16)

    def q_wait(xs, t):
        rows = pl.ds(pl.multiple_of(t * TB, TB), TB)
        pltpu.make_async_copy(qst.at[0, rows], qmy.at[xs, rows], q_r.at[xs, t]).wait()

    @pl.loop(0, T)
    def _(t):
        for xs in range(4):
            q_wait(xs, t)

    part = pl.ds(pl.multiple_of((zh * 2 + core) * 32, 32), 32)

    def go_copy():
        return remote(gout, grecv.at[x, part], go_s.at[0], go_r.at[ctx], (jnp.int32(0), head))

    def go_local():
        return pltpu.make_async_copy(gout, grecv.at[x, part], go_r.at[0])

    def o_copy(u):
        xs = (x + 3 - u // GROUPS) % 4
        piece = u % GROUPS
        rows = pl.ds(pl.multiple_of(piece * GROUP, GROUP), GROUP)
        return remote(
            ost.at[xs, rows], o_ref.at[x, rows], o_s.at[u], o_r.at[x, piece], dev(x=xs)
        )

    def o_local(u):
        piece = u % GROUPS
        rows = pl.ds(pl.multiple_of(piece * GROUP, GROUP), GROUP)
        return pltpu.make_async_copy(ost.at[x, rows], o_ref.at[x, rows], o_r.at[x, piece])

    def one_row(xs, row):
        block = run_of(zh, xs, core) * 16 + row
        q = qmy[xs, pl.ds(pl.multiple_of(row * BLK, BLK), BLK)]
        ids = [(block + NB - 1) % NB, block, (block + 1) % NB, 0, 1]
        for j in range(3):
            ids.append(ps_ref[j, x, block] * 16 + pb_ref[j, x, block])
        pairs = jnp.concatenate([kv[i] for i in ids], axis=0)
        keys, values = pairs[:, :HD], pairs[:, HD:]
        s = lax.dot_general(
            q, keys, (((1,), (1,)), ((), ())), preferred_element_type=jnp.float32
        )
        e = jnp.exp2((s - jnp.max(s, axis=1, keepdims=True)) * SCALE2)
        total = jnp.sum(e, axis=1, keepdims=True)
        out = jnp.dot(e.astype(jnp.bfloat16), values, preferred_element_type=jnp.float32)
        ost[xs, pl.ds(pl.multiple_of(row * BLK, BLK), BLK)] = (out / total).astype(jnp.bfloat16)

    @pl.loop(0, 4 * GROUPS + 1)
    def _(u):
        @pl.when(u < 4 * GROUPS)
        def _():
            xs = (x + 3 - u // GROUPS) % 4
            for k in range(GROUP // BLK):
                one_row(xs, (u % GROUPS) * (GROUP // BLK) + k)

        @pl.when((u >= 1) & (u - 1 < 3 * GROUPS))
        def _():
            o_copy(u - 1).start()

        @pl.when(u - 1 >= 3 * GROUPS)
        def _():
            o_local(u - 1).start()

        @pl.when((u == 0) & (ctx != 0))
        def _():
            go_copy().start()

        @pl.when((u == 0) & (ctx == 0))
        def _():
            go_local().start()

    for h in range(4):
        for piece in range(GROUPS):
            rows = pl.ds(piece * GROUP, GROUP)
            pltpu.make_async_copy(ost.at[0, rows], o_ref.at[h, rows], o_r.at[h, piece]).wait()

    @pl.when(ctx == 0)
    def _():
        for source in range(16):
            rows = pl.ds(((source // 8) * 2 + source % 2) * 32, 32)
            pltpu.make_async_copy(gout, grecv.at[(source // 2) % 4, rows], go_r.at[source]).wait()
        for h in range(4):
            o_ref[h, 0:128] = grecv[h]
        for target in range(1, 16):
            gq_copy(target).wait_send()

    @pl.when(ctx != 0)
    def _():
        go_copy().wait_send()

    @pl.loop(0, T)
    def _(t):
        for kind in range(3):
            ag(kind, head, t, dev_up).wait_send()
        for kind in range(3, 5):
            ag(kind, other + y, t, dev_up).wait_send()
        a, b = fwd(t)
        a.wait_send()
        b.wait_send()
        for j in range(1, 4):
            q_send(j, t).wait_send()
            kv_send(j, t).wait_send()
        for xs in range(4):
            z_fwd(xs, t).wait_send()
            c_fwd(zh, 0, xs, t).wait_send()
            c_fwd(1 - zh, 1, xs, t).wait_send()

    @pl.loop(0, 3 * GROUPS)
    def _(u):
        o_copy(u).wait_send()


def per_device(tokens, proj_weight, partner_shard, partner_block):
    bf = jnp.bfloat16
    dma = pltpu.SemaphoreType.DMA
    vmem = pl.BlockSpec(memory_space=pltpu.VMEM)
    hbm = pl.BlockSpec(memory_space=pl.ANY)
    smem = pl.BlockSpec(memory_space=pltpu.SMEM)
    out = pl.pallas_call(
        kernel,
        out_shape=jax.ShapeDtypeStruct((4, RUN, HD), bf),
        in_specs=[hbm, hbm, smem, smem],
        out_specs=vmem,
        scratch_shapes=[
            pltpu.VMEM((8, RUN, 512), bf),
            pltpu.VMEM((2, 512, 4, 384), bf),
            pltpu.VMEM((4096, 1536), bf),
            pltpu.VMEM((4, RUN, HD), bf),
            pltpu.VMEM((4, RUN // BLK, BLK, 2 * HD), bf),
            pltpu.VMEM((4, RUN, HD), bf),
            pltpu.VMEM((NB, BLK, 2 * HD), bf),
            pltpu.VMEM((32, HD), bf),
            pltpu.VMEM((32, HD), jnp.float32),
            pltpu.VMEM((32, HD), jnp.float32),
            pltpu.VMEM((32, HD), jnp.float32),
            pltpu.VMEM((32, HD), bf),
            pltpu.VMEM((4, HD, HD), bf),
            pltpu.VMEM((4, RUN, HD), bf),
            dma((1,)),
            dma((2,)),
            dma((7, T)),
            dma((8, T)),
            dma((4, T)),
            dma((4, T)),
            dma((4, T)),
            dma((4, T)),
            dma((4, T)),
            dma((4, T)),
            dma((8, T)),
            dma((8, T)),
            dma((16,)),
            dma((1,)),
            dma((1,)),
            dma((16,)),
            dma((4 * GROUPS,)),
            dma((4, GROUPS)),
        ],
        compiler_params=pltpu.CompilerParams(
            collective_id=0, has_side_effects=True, vmem_limit_bytes=60 << 20
        ),
        name="bigbird",
    )(
        tokens,
        proj_weight,
        jnp.transpose(partner_shard, (2, 0, 1)),
        jnp.transpose(partner_block, (2, 0, 1)),
    )
    return jnp.transpose(out, (1, 0, 2))


def solution(mesh):
    return jax.shard_map(
        per_device,
        mesh=mesh,
        in_specs=(P("ctx", "head"), P(None, "head", None), P("head"), P("head")),
        out_specs=P("ctx", "head", None),
        check_vma=False,
    )
```
